1024 devices in a mesh: amp: 64 (over x_lo, z, core), int: 16 (over y, x_hi).
Axes of the slice: x: 4 (x_hi: 2, x_lo: 2; x = x_hi * 2 + x_lo), y: 8, z: 16, core: 2. Of those that a mesh axis runs over, the one named last changes fastest.
Arguments:
- amps: bfloat16 [512, 16, 1000], P('amp', 'int'), may hold values from -6 to 6
- integrals: bfloat16 [65536, 16, 1000], P('amp', 'int'), may hold values from -0.125 to 0.125
- irrep_sizes: int32 [8], replicated, may hold values from 1 to 200, 1000 in all
- c_irreps: int32 [16], P('int'), may hold values from 0 to 7
Outputs:
- ladder: float32 [512, 65536], P('int', 'amp')
The draws below stay inside these ranges and needn't reach their ends.
Inputs may be any that keep to these rules, and one draw needn't show every extreme that they name: `irrep_sizes`: the sizes sum to 1000 and the largest is exactly 200.
All inputs are finite; a program needn't handle non-finite values.
Results may differ from the reference program's by a relative error of at most 0.0003.
Values may be sent and summed in bfloat16 or wider, within the bound.
No kernel may reach another device: no remote copies, remote signals or barrier semaphores. Data moves between devices by JAX's collectives and lax.ppermute only.
A program may use at most 32 MiB of HBM per device.

```python
import math
import jax
import jax.numpy as jnp
import numpy as np
from jax import lax

NV = 1000
NIRR = 8
MOST = 200
AB_DEV = 1024
NC = 16
NIJ = 512
NAB = 65536


def set_ends(values, key, low, largest):
    place = [jax.random.randint(jax.random.fold_in(key, axis), (), 0, length) for axis, length in enumerate(values.shape)]
    longest = values.shape.index(max(values.shape))
    beside = place[:longest] + [(place[longest] + 1) % values.shape[longest]] + place[longest + 1:]
    return values.at[tuple(place)].set(low).at[tuple(beside)].set(largest)


def with_spikes(drawn, rng, source, target, blocks, factor):
    def block_of(position):
        return (jnp.arange(drawn.shape[position]) // (drawn.shape[position] // blocks)).reshape((-1,) + (1,) * (drawn.ndim - 1 - position))

    near = jax.random.permutation(rng, blocks)[block_of(target)]
    other_side = (block_of(target) + blocks // 2) % blocks
    return jnp.where((block_of(source) == near) | (block_of(source) == other_side), factor * drawn, drawn)


def block_levels(rng, dims, split, least, top_value):
    def one(dim, blocks):
        heights = jax.random.uniform(jax.random.fold_in(jax.random.fold_in(rng, 6), dim), (blocks,), jnp.float32, least / len(split), top_value / len(split))
        return jnp.repeat(jnp.exp(heights), dims[dim] // blocks).reshape((-1,) + (1,) * (len(dims) - dim - 1))

    factor_of = one(*split[0])
    for cut in split[1:]:
        factor_of = factor_of * one(*cut)
    return factor_of


def length_profile(amount, total, most, skew):
    weights = [(1 << 20) // math.isqrt(grade ** skew) + 1 for grade in range(2, amount + 1)]
    surplus, given = total - most - (amount - 1), [1] * (amount - 1)
    while surplus > 0:
        candidates = [i for i in range(amount - 1) if given[i] < most]
        pool, budget = sum([weights[i] for i in candidates]), surplus
        for i in candidates:
            addition = min(most - given[i], max(1, budget * weights[i] // pool), surplus)
            given[i] = given[i] + addition
            surplus = surplus - addition
    return np.array([most] + given)


def uneven_parts(own_key, count, total, bound, skew):
    if count == 2:
        one = jax.random.randint(own_key, (), max(1, total - bound), min(bound, total - 1) + 1)
        return jnp.stack([one, total - one])
    lengths = jnp.asarray(length_profile(count, total, bound, skew), jnp.int32)
    couples = (count - 1) // 2
    donor, taker = lengths[1:1 + 2 * couples:2], lengths[2:2 + 2 * couples:2]
    room = jnp.minimum(donor - 1, bound - taker)
    moved = jax.random.randint(jax.random.fold_in(own_key, 1), (couples,), 0, 1 << 20) % (room + 1)
    lengths = lengths.at[1:1 + 2 * couples:2].set(donor - moved).at[2:2 + 2 * couples:2].set(taker + moved)
    return lengths[jax.random.permutation(jax.random.fold_in(own_key, 2), count)]


def bell_draw(stream_key, dims, deviation, limit, shards=(), kind=jnp.bfloat16):
    gain = block_levels(stream_key, dims, shards, -0.22, 0.18) if shards else 1.0
    result = jax.random.normal(stream_key, dims, jnp.float32) * deviation * gain
    return jnp.minimum(jnp.maximum(result, -limit), limit).astype(kind)


def bell_draw_with(rng, extent, deviation, most, pieces, heavy, kind=jnp.bfloat16):
    drawn = deviation * jax.random.normal(rng, extent, jnp.float32)
    if pieces:
        drawn = drawn * block_levels(rng, extent, pieces, -0.22, 0.18)
    return jnp.clip(with_spikes(drawn, jax.random.fold_in(rng, 3), *heavy), -most, most).astype(kind)


def setup_inputs(seed: int = 0) -> dict:
    seeds = jax.random.split(jax.random.key(seed), 5)
    amps = bell_draw_with(seeds[0], (NIJ, NC, NV), 1.0, 6.0, ((0, 64), (1, 16)), (1, 0, 16, 2.0))
    integrals = bell_draw(seeds[1], (NAB, NC, NV), (NC * NV // NIRR) ** -0.5, 0.125, ((0, 64), (1, 16)))
    irrep_sizes = uneven_parts(seeds[2], NIRR, NV, MOST, 2).astype(jnp.int32)
    c_irreps = set_ends(jax.random.randint(seeds[3], (NC,), 0, NIRR), jax.random.fold_in(seeds[3], 1), 0, NIRR - 1).astype(jnp.int32)
    return {"amps": amps, "integrals": integrals, "irrep_sizes": irrep_sizes, "c_irreps": c_irreps}


def allowed_mask(irrep_sizes, c_irreps, width):
    ends = jnp.cumsum(irrep_sizes)
    column = jnp.arange(width, dtype=jnp.int32)
    d_irrep = jnp.sum((column[:, None] >= ends[None, :]).astype(jnp.int32), axis=1)
    return (d_irrep[None, :] == c_irreps[:, None]).astype(jnp.bfloat16)


def reference(amps, integrals, irrep_sizes, c_irreps):
    allowed = allowed_mask(irrep_sizes, c_irreps, NV)
    blocked = (amps * allowed[None, :, :]).astype(jnp.float32).reshape(NIJ, NC * NV)
    blocks = integrals.reshape(NAB // AB_DEV, AB_DEV, NC * NV)

    def one_block(block):
        return lax.dot_general(blocked, block.astype(jnp.float32), (((1,), (1,)), ((), ())), preferred_element_type=jnp.float32)

    parts = lax.map(one_block, blocks)
    return jnp.transpose(parts, (1, 0, 2)).reshape(NIJ, NAB)
```

```python
import functools

import jax
import jax.numpy as jnp
from jax import lax
from jax.experimental import pallas as pl
from jax.experimental.pallas import tpu as pltpu
from jax.sharding import Mesh, PartitionSpec as P

WIDTH = 208
LANES = 256
VMEM = pl.BlockSpec(memory_space=pltpu.VMEM)
SMEM = pl.BlockSpec(memory_space=pltpu.SMEM)
ANY = pl.BlockSpec(memory_space=pl.ANY)


def window_of(sizes_ref, irrep_ref, width):
    g = irrep_ref[0]
    first = jnp.int32(0)
    size = jnp.int32(0)
    for k in range(sizes_ref.shape[0]):
        first = first + jnp.where(k < g, sizes_ref[k], 0)
        size = size + jnp.where(k == g, sizes_ref[k], 0)
    start = jnp.minimum((first // 8) * 8, width - WIDTH)
    return first, first + size, start


def prepare_kernel(sizes_ref, irrep_ref, amps_ref, ints_ref, window_ref, compact_ref, wide, sem):
    width = amps_ref.shape[1]
    first, last, start = window_of(sizes_ref, irrep_ref, width)
    copy = pltpu.make_async_copy(
        ints_ref.at[pl.ds(pl.multiple_of(start, 8), WIDTH), :], window_ref, sem
    )
    copy.start()
    wide[:, :width] = amps_ref[...].astype(jnp.float32)
    total = wide.shape[1]
    moved = pltpu.roll(wide[...], total - start, axis=1)[:, :LANES]
    d = lax.broadcasted_iota(jnp.int32, moved.shape, 1) + start
    moved = jnp.where((d >= first) & (d < last), moved, 0.0).astype(jnp.bfloat16)
    for j in range(compact_ref.shape[0]):
        compact_ref[j] = moved
    copy.wait()


def encode(values):
    top = jnp.max(jnp.abs(values), axis=1, keepdims=True)
    eighths = jnp.ceil(jnp.log2(jnp.maximum(top, 1e-33)) * 8.0) + 1.0
    scaled = values * (32767.0 * jnp.exp2(eighths * -0.125))
    return jnp.round(scaled).astype(jnp.int32).astype(jnp.int16), eighths


def multiply_kernel(rows_ref, own_ref, other_ref, coded_ref):
    me = lax.axis_index("x_hi")
    total = None
    for side, ints in ((me, own_ref), (1 - me, other_ref)):
        pieces = [
            rows_ref[x_lo, side, core, z]
            for x_lo in range(2)
            for q in range(4)
            for z in (2 * q, 2 * q + 1)
            for core in range(2)
        ]
        rows = jnp.concatenate(pieces, axis=0)[:, :WIDTH]
        term = jnp.dot(rows, ints[...], preferred_element_type=jnp.float32)
        total = term if total is None else total + term
    codes, eighths = encode(total)
    share = total.shape[0] // 8
    tiles = total.shape[1] // 128
    for y in range(8):
        scales = jnp.zeros((8, 128), jnp.float32)
        lane = lax.broadcasted_iota(jnp.int32, (8, 128), 1) // 32
        for t in range(share // 8):
            at = y * share + t * 8
            for u in range(tiles):
                coded_ref[y, pl.ds((t * tiles + u) * 8, 8), :] = codes[at : at + 8, u * 128 : (u + 1) * 128]
            scales = jnp.where(lane == t, eighths[at : at + 8], scales)
        coded_ref[y, pl.ds(share * tiles, 8), :] = scales.astype(jnp.int32).astype(jnp.int16)


def add_kernel(coded_ref, out_ref):
    share, columns = out_ref.shape
    tiles = columns // 128
    totals = {}
    for s in range(coded_ref.shape[0]):
        scales = coded_ref[s, pl.ds(share * tiles, 8), :].astype(jnp.int32).astype(jnp.float32)
        scales = jnp.exp2(scales * 0.125) * (1.0 / 32767.0)
        for t in range(share // 8):
            scale = scales[:, t * 32 : t * 32 + 1]
            for u in range(tiles):
                part = coded_ref[s, pl.ds((t * tiles + u) * 8, 8), :]
                part = part.astype(jnp.int32).astype(jnp.float32) * scale
                totals[t, u] = part if s == 0 else totals[t, u] + part
    for (t, u), value in totals.items():
        out_ref[pl.ds(t * 8, 8), pl.ds(u * 128, 128)] = value


def body(amps, integrals, irrep_sizes, c_irreps):
    n, _, width = amps.shape
    columns = integrals.shape[0]
    amps = amps.reshape(n, width)
    ints = jnp.transpose(integrals.reshape(columns, width))
    window, compact = pl.pallas_call(
        prepare_kernel,
        out_shape=(
            jax.ShapeDtypeStruct((WIDTH, columns), jnp.bfloat16),
            jax.ShapeDtypeStruct((16, n, LANES), jnp.bfloat16),
        ),
        in_specs=[SMEM, SMEM, VMEM, ANY],
        out_specs=(VMEM, VMEM),
        scratch_shapes=[pltpu.VMEM((n, 1024), jnp.float32), pltpu.SemaphoreType.DMA],
        name="prepare",
    )(irrep_sizes, c_irreps, amps, ints)
    other = lax.ppermute(window, "x_hi", [(0, 1), (1, 0)])
    column = lax.all_to_all(compact, "z", 0, 0, tiled=True)
    halves = column.reshape(4, 2, 2, n, LANES).transpose(1, 0, 2, 3, 4).reshape(1, 2, 1, 8, n, LANES)
    halves = jnp.broadcast_to(halves, (2, 2, 2, 8, n, LANES)).reshape(8, 8, n, LANES)
    rows = lax.all_to_all(halves, ("x_lo", "x_hi", "core"), 0, 0, tiled=True)
    rows = rows.reshape(2, 2, 2, 8, n, LANES)
    share = 32
    length = share * columns // 128 + 8
    coded = pl.pallas_call(
        multiply_kernel,
        out_shape=jax.ShapeDtypeStruct((8, length, 128), jnp.int16),
        in_specs=[VMEM, VMEM, VMEM],
        out_specs=VMEM,
        name="multiply",
    )(rows, window, other)
    coded = lax.all_to_all(coded, "y", 0, 0, tiled=True)
    return pl.pallas_call(
        add_kernel,
        out_shape=jax.ShapeDtypeStruct((share, columns), jnp.float32),
        in_specs=[VMEM],
        out_specs=VMEM,
        name="add",
    )(coded)


def solution(mesh):
    fine = Mesh(mesh.devices.reshape(2, 16, 2, 8, 2), ("x_lo", "z", "core", "y", "x_hi"))
    amp, inter = ("x_lo", "z", "core"), ("y", "x_hi")
    placed = (P(amp, inter, None), P(amp, inter, None), P(), P(inter))
    return jax.shard_map(
        body, mesh=fine, in_specs=placed, out_specs=P(inter, amp), check_vma=False
    )
```

```python
import functools

import jax
import jax.numpy as jnp
from jax import lax
from jax.experimental import pallas as pl
from jax.experimental.pallas import tpu as pltpu
from jax.sharding import Mesh, PartitionSpec as P

WIDTH = 208
LANES = 256
VMEM = pl.BlockSpec(memory_space=pltpu.VMEM)
HBM = pl.BlockSpec(memory_space=pltpu.HBM)
SMALL = pltpu.CompilerParams(vmem_limit_bytes=8 << 20)


def window_of(sizes_ref, irrep_ref, width):
    g = irrep_ref[0]
    first = jnp.int32(0)
    size = jnp.int32(0)
    for k in range(sizes_ref.shape[0]):
        first = first + jnp.where(k < g, sizes_ref[k], 0)
        size = size + jnp.where(k == g, sizes_ref[k], 0)
    start = jnp.minimum((first // 8) * 8, width - WIDTH)
    return first, first + size, start


def prepare_kernel(sizes_hbm, irrep_hbm, amps_hbm, ints_hbm, window_ref, compact_ref, sizes_ref, irrep_ref, amps_ref, wide, sems):
    width = amps_hbm.shape[1]
    sizes_copy = pltpu.make_async_copy(sizes_hbm, sizes_ref, sems.at[0])
    irrep_copy = pltpu.make_async_copy(irrep_hbm, irrep_ref, sems.at[1])
    amps_copy = pltpu.make_async_copy(amps_hbm, amps_ref, sems.at[2])
    sizes_copy.start()
    irrep_copy.start()
    amps_copy.start()
    sizes_copy.wait()
    irrep_copy.wait()
    first, last, start = window_of(sizes_ref, irrep_ref, width)
    window_copy = pltpu.make_async_copy(
        ints_hbm.at[pl.ds(pl.multiple_of(start, 8), WIDTH), :], window_ref, sems.at[3]
    )
    window_copy.start()
    amps_copy.wait()
    wide[:, :width] = amps_ref[...].astype(jnp.float32)
    total = wide.shape[1]
    moved = pltpu.roll(wide[...], total - start, axis=1)[:, :LANES]
    d = lax.broadcasted_iota(jnp.int32, moved.shape, 1) + start
    moved = jnp.where((d >= first) & (d < last), moved, 0.0).astype(jnp.bfloat16)
    for j in range(compact_ref.shape[0]):
        compact_ref[j] = moved
    window_copy.wait()


def encode(values):
    top = jnp.max(jnp.abs(values), axis=1, keepdims=True)
    eighths = jnp.ceil(jnp.log2(jnp.maximum(top, 1e-33)) * 8.0) + 1.0
    scaled = values * (32767.0 * jnp.exp2(eighths * -0.125))
    return jnp.round(scaled).astype(jnp.int32).astype(jnp.int16), eighths


def multiply_kernel(rows_ref, own_ref, other_ref, coded_ref):
    me = lax.axis_index("x_hi")
    total = None
    for side, ints in ((me, own_ref), (1 - me, other_ref)):
        pieces = [
            rows_ref[x_lo, side, core, z]
            for x_lo in range(2)
            for q in range(4)
            for z in (2 * q, 2 * q + 1)
            for core in range(2)
        ]
        rows = jnp.concatenate(pieces, axis=0)[:, :WIDTH]
        term = jnp.dot(rows, ints[...], preferred_element_type=jnp.float32)
        total = term if total is None else total + term
    codes, eighths = encode(total)
    share = total.shape[0] // 8
    tiles = total.shape[1] // 128
    for y in range(8):
        scales = jnp.zeros((8, 128), jnp.float32)
        lane = lax.broadcasted_iota(jnp.int32, (8, 128), 1) // 32
        for t in range(share // 8):
            at = y * share + t * 8
            for u in range(tiles):
                coded_ref[y, pl.ds((t * tiles + u) * 8, 8), :] = codes[at : at + 8, u * 128 : (u + 1) * 128]
            scales = jnp.where(lane == t, eighths[at : at + 8], scales)
        coded_ref[y, pl.ds(share * tiles, 8), :] = scales.astype(jnp.int32).astype(jnp.int16)


def add_kernel(coded_ref, out_ref):
    share, columns = out_ref.shape
    tiles = columns // 128
    totals = {}
    for s in range(coded_ref.shape[0]):
        scales = coded_ref[s, pl.ds(share * tiles, 8), :].astype(jnp.int32).astype(jnp.float32)
        scales = jnp.exp2(scales * 0.125) * (1.0 / 32767.0)
        for t in range(share // 8):
            scale = scales[:, t * 32 : t * 32 + 1]
            for u in range(tiles):
                part = coded_ref[s, pl.ds((t * tiles + u) * 8, 8), :]
                part = part.astype(jnp.int32).astype(jnp.float32) * scale
                totals[t, u] = part if s == 0 else totals[t, u] + part
    for (t, u), value in totals.items():
        out_ref[pl.ds(t * 8, 8), pl.ds(u * 128, 128)] = value


def body(amps, integrals, irrep_sizes, c_irreps):
    n, _, width = amps.shape
    columns = integrals.shape[0]
    amps = amps.reshape(n, width)
    ints = jnp.transpose(integrals.reshape(columns, width))
    window, compact = pl.pallas_call(
        prepare_kernel,
        out_shape=(
            jax.ShapeDtypeStruct((WIDTH, columns), jnp.bfloat16),
            jax.ShapeDtypeStruct((16, n, LANES), jnp.bfloat16),
        ),
        in_specs=[HBM] * 4,
        out_specs=(VMEM, VMEM),
        scratch_shapes=[
            pltpu.SMEM(irrep_sizes.shape, jnp.int32),
            pltpu.SMEM(c_irreps.shape, jnp.int32),
            pltpu.VMEM(amps.shape, amps.dtype),
            pltpu.VMEM((n, 1024), jnp.float32),
            pltpu.SemaphoreType.DMA((4,)),
        ],
        compiler_params=SMALL,
        name="prepare",
    )(irrep_sizes, c_irreps, amps, ints)
    other = lax.ppermute(window, "x_hi", [(0, 1), (1, 0)])
    column = lax.all_to_all(compact, "z", 0, 0, tiled=True)
    halves = column.reshape(4, 2, 2, n, LANES).transpose(1, 0, 2, 3, 4).reshape(1, 2, 1, 8, n, LANES)
    halves = jnp.broadcast_to(halves, (2, 2, 2, 8, n, LANES)).reshape(8, 8, n, LANES)
    rows = lax.all_to_all(halves, ("x_lo", "x_hi", "core"), 0, 0, tiled=True)
    rows = rows.reshape(2, 2, 2, 8, n, LANES)
    share = 32
    length = share * columns // 128 + 8
    coded = pl.pallas_call(
        multiply_kernel,
        out_shape=jax.ShapeDtypeStruct((8, length, 128), jnp.int16),
        in_specs=[VMEM, VMEM, VMEM],
        out_specs=VMEM,
        compiler_params=SMALL,
        name="multiply",
    )(rows, window, other)
    coded = lax.all_to_all(coded, "y", 0, 0, tiled=True)
    return pl.pallas_call(
        add_kernel,
        out_shape=jax.ShapeDtypeStruct((share, columns), jnp.float32),
        in_specs=[VMEM],
        out_specs=VMEM,
        compiler_params=SMALL,
        name="add",
    )(coded)


def solution(mesh):
    fine = Mesh(mesh.devices.reshape(2, 16, 2, 8, 2), ("x_lo", "z", "core", "y", "x_hi"))
    amp, inter = ("x_lo", "z", "core"), ("y", "x_hi")
    placed = (P(amp, inter, None), P(amp, inter, None), P(), P(inter))
    return jax.shard_map(
        body, mesh=fine, in_specs=placed, out_specs=P(inter, amp), check_vma=False
    )
```

```python
import functools

import jax
import jax.numpy as jnp
from jax import lax
from jax.experimental import pallas as pl
from jax.experimental.pallas import tpu as pltpu
from jax.sharding import Mesh, PartitionSpec as P

Z_ORDER = [(12 + j) % 16 for j in range(16)]
Y_ORDER = [(4 + j) % 8 for j in range(8)]
X_FIRST = 7
WIDTH = 208
LANES = 256
VMEM = pl.BlockSpec(memory_space=pltpu.VMEM)
SMEM = pl.BlockSpec(memory_space=pltpu.SMEM)
HBM = pl.BlockSpec(memory_space=pltpu.HBM)
SMALL = pltpu.CompilerParams(vmem_limit_bytes=8 << 20)


def window_of(sizes_ref, irrep_ref, width):
    g = irrep_ref[0]
    first = jnp.int32(0)
    size = jnp.int32(0)
    for k in range(sizes_ref.shape[0]):
        first = first + jnp.where(k < g, sizes_ref[k], 0)
        size = size + jnp.where(k == g, sizes_ref[k], 0)
    start = jnp.minimum((first // 8) * 8, width - WIDTH)
    return first, first + size, start


def compact_kernel(irrep_ref, sizes_hbm, amps_hbm, compact_ref, sizes_ref, amps_ref, wide, sems):
    width = amps_hbm.shape[1]
    sizes_copy = pltpu.make_async_copy(sizes_hbm, sizes_ref, sems.at[0])
    amps_copy = pltpu.make_async_copy(amps_hbm, amps_ref, sems.at[1])
    sizes_copy.start()
    amps_copy.start()
    sizes_copy.wait()
    first, last, start = window_of(sizes_ref, irrep_ref, width)
    amps_copy.wait()
    wide[:, :width] = amps_ref[...].astype(jnp.float32)
    total = wide.shape[1]
    moved = pltpu.roll(wide[...], total - start, axis=1)[:, :LANES]
    d = lax.broadcasted_iota(jnp.int32, moved.shape, 1) + start
    moved = jnp.where((d >= first) & (d < last), moved, 0.0).astype(jnp.bfloat16)
    for j in range(compact_ref.shape[0]):
        compact_ref[j] = moved


def window_kernel(irrep_ref, sizes_hbm, ints_hbm, window_ref, sizes_ref, sems):
    sizes_copy = pltpu.make_async_copy(sizes_hbm, sizes_ref, sems.at[0])
    sizes_copy.start()
    sizes_copy.wait()
    _, _, start = window_of(sizes_ref, irrep_ref, ints_hbm.shape[0])
    window_copy = pltpu.make_async_copy(
        ints_hbm.at[pl.ds(pl.multiple_of(start, 8), WIDTH), :], window_ref, sems.at[1]
    )
    window_copy.start()
    window_copy.wait()


def spread_kernel(column_ref, halves_ref):
    for j in range(8):
        x_hi = ((j ^ X_FIRST) >> 1) & 1
        for i in range(8):
            halves_ref[j, i] = column_ref[Z_ORDER.index((i >> 1) * 4 + x_hi * 2 + (i & 1))]


def encode(values):
    top = jnp.max(jnp.abs(values), axis=1, keepdims=True)
    eighths = jnp.ceil(jnp.log2(jnp.maximum(top, 1e-33)) * 8.0) + 1.0
    scaled = values * (32767.0 * jnp.exp2(eighths * -0.125))
    return jnp.round(scaled).astype(jnp.int32).astype(jnp.int16), eighths


def multiply_kernel(rows_ref, own_ref, other_ref, coded_ref):
    me = lax.axis_index("x_hi")
    total = None
    for side, ints in ((me, own_ref), (1 - me, other_ref)):
        pieces = [
            rows_ref[((x_lo * 4 + core) ^ X_FIRST) ^ (2 * side), 2 * q + low]
            for x_lo in range(2)
            for q in range(4)
            for low in range(2)
            for core in range(2)
        ]
        rows = jnp.concatenate(pieces, axis=0)[:, :WIDTH]
        term = jnp.dot(rows, ints[...], preferred_element_type=jnp.float32)
        total = term if total is None else total + term
    codes, eighths = encode(total)
    share = total.shape[0] // 8
    tiles = total.shape[1] // 128
    for y in range(8):
        scales = jnp.zeros((8, 128), jnp.float32)
        lane = lax.broadcasted_iota(jnp.int32, (8, 128), 1) // 32
        for t in range(share // 8):
            at = y * share + t * 8
            for u in range(tiles):
                coded_ref[Y_ORDER.index(y), pl.ds((t * tiles + u) * 8, 8), :] = codes[at : at + 8, u * 128 : (u + 1) * 128]
            scales = jnp.where(lane == t, eighths[at : at + 8], scales)
        coded_ref[Y_ORDER.index(y), pl.ds(share * tiles, 8), :] = scales.astype(jnp.int32).astype(jnp.int16)


def add_kernel(coded_ref, out_ref):
    share, columns = out_ref.shape
    tiles = columns // 128
    totals = {}
    for s in range(coded_ref.shape[0]):
        scales = coded_ref[s, pl.ds(share * tiles, 8), :].astype(jnp.int32).astype(jnp.float32)
        scales = jnp.exp2(scales * 0.125) * (1.0 / 32767.0)
        for t in range(share // 8):
            scale = scales[:, t * 32 : t * 32 + 1]
            for u in range(tiles):
                part = coded_ref[s, pl.ds((t * tiles + u) * 8, 8), :]
                part = part.astype(jnp.int32).astype(jnp.float32) * scale
                totals[t, u] = part if s == 0 else totals[t, u] + part
    for (t, u), value in totals.items():
        out_ref[pl.ds(t * 8, 8), pl.ds(u * 128, 128)] = value


def exchange(x, axis, order):
    return lax.all_to_all(x, axis, 0, 0, axis_index_groups=[order], tiled=True)


def body(amps, integrals, irrep_sizes, c_irreps):
    n, _, width = amps.shape
    columns = integrals.shape[0]
    amps = amps.reshape(n, width)
    ints = jnp.transpose(integrals.reshape(columns, width))
    sizes, amps, ints = (pltpu.with_memory_space_constraint(a, pltpu.HBM) for a in (irrep_sizes, amps, ints))
    compact = pl.pallas_call(
        compact_kernel,
        out_shape=jax.ShapeDtypeStruct((16, n, LANES), jnp.bfloat16),
        in_specs=[SMEM, HBM, HBM],
        out_specs=VMEM,
        scratch_shapes=[
            pltpu.SMEM(irrep_sizes.shape, jnp.int32),
            pltpu.VMEM(amps.shape, amps.dtype),
            pltpu.VMEM((n, 1024), jnp.float32),
            pltpu.SemaphoreType.DMA((2,)),
        ],
        compiler_params=SMALL,
        name="compact",
    )(c_irreps, sizes, amps)
    window = pl.pallas_call(
        window_kernel,
        out_shape=jax.ShapeDtypeStruct((WIDTH, columns), jnp.bfloat16),
        in_specs=[SMEM, HBM, HBM],
        out_specs=VMEM,
        scratch_shapes=[pltpu.SMEM(irrep_sizes.shape, jnp.int32), pltpu.SemaphoreType.DMA((2,))],
        compiler_params=SMALL,
        name="window",
    )(c_irreps, sizes, ints)
    other = lax.ppermute(window, "x_hi", [(0, 1), (1, 0)])
    column = exchange(compact, "z", Z_ORDER)
    halves = pl.pallas_call(
        spread_kernel,
        out_shape=jax.ShapeDtypeStruct((8, 8, n, LANES), jnp.bfloat16),
        in_specs=[VMEM],
        out_specs=VMEM,
        compiler_params=SMALL,
        name="spread",
    )(column)
    rows = exchange(halves, ("x_lo", "x_hi", "core"), [j ^ X_FIRST for j in range(8)])
    share = 32
    length = share * columns // 128 + 8
    coded = pl.pallas_call(
        multiply_kernel,
        out_shape=jax.ShapeDtypeStruct((8, length, 128), jnp.int16),
        in_specs=[VMEM, VMEM, VMEM],
        out_specs=VMEM,
        compiler_params=SMALL,
        name="multiply",
    )(rows, window, other)
    coded = exchange(coded, "y", Y_ORDER)
    return pl.pallas_call(
        add_kernel,
        out_shape=jax.ShapeDtypeStruct((share, columns), jnp.float32),
        in_specs=[VMEM],
        out_specs=VMEM,
        compiler_params=SMALL,
        name="add",
    )(coded)


def solution(mesh):
    fine = Mesh(mesh.devices.reshape(2, 16, 2, 8, 2), ("x_lo", "z", "core", "y", "x_hi"))
    amp, inter = ("x_lo", "z", "core"), ("y", "x_hi")
    placed = (P(amp, inter, None), P(amp, inter, None), P(), P(inter))
    return jax.shard_map(
        body, mesh=fine, in_specs=placed, out_specs=P(inter, amp), check_vma=False
    )
```

```python
import functools

import jax
import jax.numpy as jnp
from jax import lax
from jax.experimental import pallas as pl
from jax.experimental.pallas import tpu as pltpu
from jax.sharding import Mesh, PartitionSpec as P

Z_ORDER = [(13 + j) % 16 for j in range(16)]
Y_ORDER = [(5 + j) % 8 for j in range(8)]
X_FIRST = 3
WIDTH = 208
LANES = 256
VMEM = pl.BlockSpec(memory_space=pltpu.VMEM)
SMEM = pl.BlockSpec(memory_space=pltpu.SMEM)
HBM = pl.BlockSpec(memory_space=pltpu.HBM)
SMALL = pltpu.CompilerParams(vmem_limit_bytes=8 << 20)


def window_of(sizes_ref, irrep_ref, width):
    g = irrep_ref[0]
    first = jnp.int32(0)
    size = jnp.int32(0)
    for k in range(sizes_ref.shape[0]):
        first = first + jnp.where(k < g, sizes_ref[k], 0)
        size = size + jnp.where(k == g, sizes_ref[k], 0)
    start = jnp.minimum((first // 8) * 8, width - WIDTH)
    return first, first + size, start


def compact_kernel(irrep_ref, sizes_hbm, amps_hbm, compact_ref, sizes_ref, amps_ref, wide, sems):
    width = amps_hbm.shape[1]
    sizes_copy = pltpu.make_async_copy(sizes_hbm, sizes_ref, sems.at[0])
    amps_copy = pltpu.make_async_copy(amps_hbm, amps_ref, sems.at[1])
    sizes_copy.start()
    amps_copy.start()
    sizes_copy.wait()
    first, last, start = window_of(sizes_ref, irrep_ref, width)
    amps_copy.wait()
    wide[:, :width] = amps_ref[...].astype(jnp.float32)
    total = wide.shape[1]
    moved = pltpu.roll(wide[...], total - start, axis=1)[:, :LANES]
    d = lax.broadcasted_iota(jnp.int32, moved.shape, 1) + start
    moved = jnp.where((d >= first) & (d < last), moved, 0.0).astype(jnp.bfloat16)
    for j in range(compact_ref.shape[0]):
        compact_ref[j] = moved


def window_kernel(irrep_ref, sizes_hbm, ints_hbm, window_ref, sizes_ref, sems):
    sizes_copy = pltpu.make_async_copy(sizes_hbm, sizes_ref, sems.at[0])
    sizes_copy.start()
    sizes_copy.wait()
    _, _, start = window_of(sizes_ref, irrep_ref, ints_hbm.shape[0])
    window_copy = pltpu.make_async_copy(
        ints_hbm.at[pl.ds(pl.multiple_of(start, 8), WIDTH), :], window_ref, sems.at[1]
    )
    window_copy.start()
    window_copy.wait()


def spread_kernel(column_ref, halves_ref):
    for j in range(8):
        x_hi = ((j ^ X_FIRST) >> 1) & 1
        for i in range(8):
            halves_ref[j, i] = column_ref[Z_ORDER.index((i >> 1) * 4 + x_hi * 2 + (i & 1))]


def encode(values):
    top = jnp.max(jnp.abs(values), axis=1, keepdims=True)
    eighths = jnp.ceil(jnp.log2(jnp.maximum(top, 1e-33)) * 8.0) + 1.0
    scaled = values * (32767.0 * jnp.exp2(eighths * -0.125))
    return jnp.round(scaled).astype(jnp.int32).astype(jnp.int16), eighths


def multiply_kernel(rows_ref, own_ref, other_ref, coded_ref):
    me = lax.axis_index("x_hi")
    total = None
    for side, ints in ((me, own_ref), (1 - me, other_ref)):
        pieces = [
            rows_ref[((x_lo * 4 + core) ^ X_FIRST) ^ (2 * side), 2 * q + low]
            for x_lo in range(2)
            for q in range(4)
            for low in range(2)
            for core in range(2)
        ]
        rows = jnp.concatenate(pieces, axis=0)[:, :WIDTH]
        term = jnp.dot(rows, ints[...], preferred_element_type=jnp.float32)
        total = term if total is None else total + term
    codes, eighths = encode(total)
    share = total.shape[0] // 8
    tiles = total.shape[1] // 128
    for y in range(8):
        scales = jnp.zeros((8, 128), jnp.float32)
        lane = lax.broadcasted_iota(jnp.int32, (8, 128), 1) // 32
        for t in range(share // 8):
            at = y * share + t * 8
            for u in range(tiles):
                coded_ref[Y_ORDER.index(y), pl.ds((t * tiles + u) * 8, 8), :] = codes[at : at + 8, u * 128 : (u + 1) * 128]
            scales = jnp.where(lane == t, eighths[at : at + 8], scales)
        coded_ref[Y_ORDER.index(y), pl.ds(share * tiles, 8), :] = scales.astype(jnp.int32).astype(jnp.int16)


def add_kernel(coded_ref, out_ref):
    share, columns = out_ref.shape
    tiles = columns // 128
    totals = {}
    for s in range(coded_ref.shape[0]):
        scales = coded_ref[s, pl.ds(share * tiles, 8), :].astype(jnp.int32).astype(jnp.float32)
        scales = jnp.exp2(scales * 0.125) * (1.0 / 32767.0)
        for t in range(share // 8):
            scale = scales[:, t * 32 : t * 32 + 1]
            for u in range(tiles):
                part = coded_ref[s, pl.ds((t * tiles + u) * 8, 8), :]
                part = part.astype(jnp.int32).astype(jnp.float32) * scale
                totals[t, u] = part if s == 0 else totals[t, u] + part
    for (t, u), value in totals.items():
        out_ref[pl.ds(t * 8, 8), pl.ds(u * 128, 128)] = value


def exchange(x, axis, order):
    return lax.all_to_all(x, axis, 0, 0, axis_index_groups=[order], tiled=True)


def body(amps, integrals, irrep_sizes, c_irreps):
    n, _, width = amps.shape
    columns = integrals.shape[0]
    amps = amps.reshape(n, width)
    ints = jnp.transpose(integrals.reshape(columns, width))
    sizes, amps, ints = (pltpu.with_memory_space_constraint(a, pltpu.HBM) for a in (irrep_sizes, amps, ints))
    compact = pl.pallas_call(
        compact_kernel,
        out_shape=jax.ShapeDtypeStruct((16, n, LANES), jnp.bfloat16),
        in_specs=[SMEM, HBM, HBM],
        out_specs=VMEM,
        scratch_shapes=[
            pltpu.SMEM(irrep_sizes.shape, jnp.int32),
            pltpu.VMEM(amps.shape, amps.dtype),
            pltpu.VMEM((n, 1024), jnp.float32),
            pltpu.SemaphoreType.DMA((2,)),
        ],
        compiler_params=SMALL,
        name="compact",
    )(c_irreps, sizes, amps)
    window = pl.pallas_call(
        window_kernel,
        out_shape=jax.ShapeDtypeStruct((WIDTH, columns), jnp.bfloat16),
        in_specs=[SMEM, HBM, HBM],
        out_specs=VMEM,
        scratch_shapes=[pltpu.SMEM(irrep_sizes.shape, jnp.int32), pltpu.SemaphoreType.DMA((2,))],
        compiler_params=SMALL,
        name="window",
    )(c_irreps, sizes, ints)
    other = lax.ppermute(window, "x_hi", [(0, 1), (1, 0)])
    column = exchange(compact, "z", Z_ORDER)
    halves = pl.pallas_call(
        spread_kernel,
        out_shape=jax.ShapeDtypeStruct((8, 8, n, LANES), jnp.bfloat16),
        in_specs=[VMEM],
        out_specs=VMEM,
        compiler_params=SMALL,
        name="spread",
    )(column)
    rows = exchange(halves, ("x_lo", "x_hi", "core"), [j ^ X_FIRST for j in range(8)])
    share = 32
    length = share * columns // 128 + 8
    coded = pl.pallas_call(
        multiply_kernel,
        out_shape=jax.ShapeDtypeStruct((8, length, 128), jnp.int16),
        in_specs=[VMEM, VMEM, VMEM],
        out_specs=VMEM,
        compiler_params=SMALL,
        name="multiply",
    )(rows, window, other)
    coded = exchange(coded, "y", Y_ORDER)
    return pl.pallas_call(
        add_kernel,
        out_shape=jax.ShapeDtypeStruct((share, columns), jnp.float32),
        in_specs=[VMEM],
        out_specs=VMEM,
        compiler_params=SMALL,
        name="add",
    )(coded)


def solution(mesh):
    fine = Mesh(mesh.devices.reshape(2, 16, 2, 8, 2), ("x_lo", "z", "core", "y", "x_hi"))
    amp, inter = ("x_lo", "z", "core"), ("y", "x_hi")
    placed = (P(amp, inter, None), P(amp, inter, None), P(), P(inter))
    return jax.shard_map(
        body, mesh=fine, in_specs=placed, out_specs=P(inter, amp), check_vma=False
    )
```

```python
import functools

import jax
import jax.numpy as jnp
from jax import lax
from jax.experimental import pallas as pl
from jax.experimental.pallas import tpu as pltpu
from jax.sharding import Mesh, PartitionSpec as P

Z_ORDER = [13, 0, 1, 4, 5, 8, 9, 12, 15, 2, 3, 6, 7, 10, 11, 14]
Y_ORDER = [(5 + j) % 8 for j in range(8)]
X_FIRST = 3
WIDTH = 208
LANES = 256
VMEM = pl.BlockSpec(memory_space=pltpu.VMEM)
SMEM = pl.BlockSpec(memory_space=pltpu.SMEM)
HBM = pl.BlockSpec(memory_space=pltpu.HBM)
SMALL = pltpu.CompilerParams(vmem_limit_bytes=8 << 20)


def window_of(sizes_ref, irrep_ref, width):
    g = irrep_ref[0]
    first = jnp.int32(0)
    size = jnp.int32(0)
    for k in range(sizes_ref.shape[0]):
        first = first + jnp.where(k < g, sizes_ref[k], 0)
        size = size + jnp.where(k == g, sizes_ref[k], 0)
    start = jnp.minimum((first // 8) * 8, width - WIDTH)
    return first, first + size, start


def compact_kernel(irrep_ref, sizes_hbm, amps_hbm, compact_ref, sizes_ref, amps_ref, wide, sems):
    width = amps_hbm.shape[1]
    sizes_copy = pltpu.make_async_copy(sizes_hbm, sizes_ref, sems.at[0])
    amps_copy = pltpu.make_async_copy(amps_hbm, amps_ref, sems.at[1])
    sizes_copy.start()
    amps_copy.start()
    sizes_copy.wait()
    first, last, start = window_of(sizes_ref, irrep_ref, width)
    amps_copy.wait()
    wide[:, :width] = amps_ref[...].astype(jnp.float32)
    total = wide.shape[1]
    moved = pltpu.roll(wide[...], total - start, axis=1)[:, :LANES]
    d = lax.broadcasted_iota(jnp.int32, moved.shape, 1) + start
    moved = jnp.where((d >= first) & (d < last), moved, 0.0).astype(jnp.bfloat16)
    for j in range(compact_ref.shape[0]):
        compact_ref[j] = moved


def window_kernel(irrep_ref, sizes_hbm, ints_hbm, window_ref, sizes_ref, sems):
    sizes_copy = pltpu.make_async_copy(sizes_hbm, sizes_ref, sems.at[0])
    sizes_copy.start()
    sizes_copy.wait()
    _, _, start = window_of(sizes_ref, irrep_ref, ints_hbm.shape[0])
    window_copy = pltpu.make_async_copy(
        ints_hbm.at[pl.ds(pl.multiple_of(start, 8), WIDTH), :], window_ref, sems.at[1]
    )
    window_copy.start()
    window_copy.wait()


def spread_kernel(column_ref, halves_hbm, sems):
    copies = []
    for j in range(8):
        x_hi = ((j ^ X_FIRST) >> 1) & 1
        copies.append(pltpu.make_async_copy(column_ref.at[pl.ds(8 * x_hi, 8)], halves_hbm.at[j], sems.at[j]))
        copies[-1].start()
    for copy in copies:
        copy.wait()


def encode(values):
    top = jnp.max(jnp.abs(values), axis=1, keepdims=True)
    eighths = jnp.ceil(jnp.log2(jnp.maximum(top, 1e-33)) * 8.0) + 1.0
    scaled = values * (32767.0 * jnp.exp2(eighths * -0.125))
    return jnp.round(scaled).astype(jnp.int32).astype(jnp.int16), eighths


def multiply_kernel(rows_ref, own_ref, other_ref, coded_ref):
    me = lax.axis_index("x_hi")
    total = None
    for side, ints in ((me, own_ref), (1 - me, other_ref)):
        pieces = [
            rows_ref[((x_lo * 4 + core) ^ X_FIRST) ^ (2 * side), (2 * q + low + 1) % 8]
            for x_lo in range(2)
            for q in range(4)
            for low in range(2)
            for core in range(2)
        ]
        rows = jnp.concatenate(pieces, axis=0)[:, :WIDTH]
        term = jnp.dot(rows, ints[...], preferred_element_type=jnp.float32)
        total = term if total is None else total + term
    codes, eighths = encode(total)
    share = total.shape[0] // 8
    tiles = total.shape[1] // 128
    for y in range(8):
        scales = jnp.zeros((8, 128), jnp.float32)
        lane = lax.broadcasted_iota(jnp.int32, (8, 128), 1) // 32
        for t in range(share // 8):
            at = y * share + t * 8
            for u in range(tiles):
                coded_ref[Y_ORDER.index(y), pl.ds((t * tiles + u) * 8, 8), :] = codes[at : at + 8, u * 128 : (u + 1) * 128]
            scales = jnp.where(lane == t, eighths[at : at + 8], scales)
        coded_ref[Y_ORDER.index(y), pl.ds(share * tiles, 8), :] = scales.astype(jnp.int32).astype(jnp.int16)


def add_kernel(coded_ref, out_hbm, out_ref, sems):
    share, columns = out_ref.shape
    tiles = columns // 128
    scales = []
    for s in range(coded_ref.shape[0]):
        marks = coded_ref[s, pl.ds(share * tiles, 8), :].astype(jnp.int32).astype(jnp.float32)
        scales.append(jnp.exp2(marks * 0.125) * (1.0 / 32767.0))
    copies = []
    for t in range(share // 8):
        totals = [None] * tiles
        for s, marks in enumerate(scales):
            scale = marks[:, t * 32 : t * 32 + 1]
            for u in range(tiles):
                part = coded_ref[s, pl.ds((t * tiles + u) * 8, 8), :]
                part = part.astype(jnp.int32).astype(jnp.float32) * scale
                totals[u] = part if totals[u] is None else totals[u] + part
        for u, value in enumerate(totals):
            out_ref[pl.ds(t * 8, 8), pl.ds(u * 128, 128)] = value
        rows = pl.ds(t * 8, 8)
        copies.append(pltpu.make_async_copy(out_ref.at[rows], out_hbm.at[rows], sems.at[t]))
        copies[-1].start()
    for copy in copies:
        copy.wait()


def exchange(x, axis, order):
    return lax.all_to_all(x, axis, 0, 0, axis_index_groups=[order], tiled=True)


def body(amps, integrals, irrep_sizes, c_irreps):
    n, _, width = amps.shape
    columns = integrals.shape[0]
    amps = amps.reshape(n, width)
    ints = jnp.transpose(integrals.reshape(columns, width))
    sizes, amps, ints = (pltpu.with_memory_space_constraint(a, pltpu.HBM) for a in (irrep_sizes, amps, ints))
    compact = pl.pallas_call(
        compact_kernel,
        out_shape=jax.ShapeDtypeStruct((16, n, LANES), jnp.bfloat16),
        in_specs=[SMEM, HBM, HBM],
        out_specs=VMEM,
        scratch_shapes=[
            pltpu.SMEM(irrep_sizes.shape, jnp.int32),
            pltpu.VMEM(amps.shape, amps.dtype),
            pltpu.VMEM((n, 1024), jnp.float32),
            pltpu.SemaphoreType.DMA((2,)),
        ],
        compiler_params=SMALL,
        name="compact",
    )(c_irreps, sizes, amps)
    window = pl.pallas_call(
        window_kernel,
        out_shape=jax.ShapeDtypeStruct((WIDTH, columns), jnp.bfloat16),
        in_specs=[SMEM, HBM, HBM],
        out_specs=VMEM,
        scratch_shapes=[pltpu.SMEM(irrep_sizes.shape, jnp.int32), pltpu.SemaphoreType.DMA((2,))],
        compiler_params=SMALL,
        name="window",
    )(c_irreps, sizes, ints)
    other = lax.ppermute(window, "x_hi", [(0, 1), (1, 0)])
    column = exchange(compact, "z", Z_ORDER)
    halves = pl.pallas_call(
        spread_kernel,
        out_shape=jax.ShapeDtypeStruct((8, 8, n, LANES), jnp.bfloat16),
        in_specs=[VMEM],
        out_specs=HBM,
        scratch_shapes=[pltpu.SemaphoreType.DMA((8,))],
        compiler_params=SMALL,
        name="spread",
    )(column)
    rows = exchange(halves, ("x_lo", "x_hi", "core"), [j ^ X_FIRST for j in range(8)])
    share = 32
    length = share * columns // 128 + 8
    coded = pl.pallas_call(
        multiply_kernel,
        out_shape=jax.ShapeDtypeStruct((8, length, 128), jnp.int16),
        in_specs=[VMEM, VMEM, VMEM],
        out_specs=VMEM,
        compiler_params=SMALL,
        name="multiply",
    )(rows, window, other)
    coded = exchange(coded, "y", Y_ORDER)
    return pl.pallas_call(
        add_kernel,
        out_shape=jax.ShapeDtypeStruct((share, columns), jnp.float32),
        in_specs=[VMEM],
        out_specs=HBM,
        scratch_shapes=[pltpu.VMEM((share, columns), jnp.float32), pltpu.SemaphoreType.DMA((share // 8,))],
        compiler_params=SMALL,
        name="add",
    )(coded)


def solution(mesh):
    fine = Mesh(mesh.devices.reshape(2, 16, 2, 8, 2), ("x_lo", "z", "core", "y", "x_hi"))
    amp, inter = ("x_lo", "z", "core"), ("y", "x_hi")
    placed = (P(amp, inter, None), P(amp, inter, None), P(), P(inter))
    return jax.shard_map(
        body, mesh=fine, in_specs=placed, out_specs=P(inter, amp), check_vma=False
    )
```

```python
import functools

import jax
import jax.numpy as jnp
from jax import lax
from jax.experimental import pallas as pl
from jax.experimental.pallas import tpu as pltpu
from jax.sharding import Mesh, PartitionSpec as P

Z_ORDER = [13, 0, 1, 4, 5, 8, 9, 12, 15, 2, 3, 6, 7, 10, 11, 14]
Y_ORDER = [(4 + j) % 8 for j in range(8)]
X_FIRST = 3
WIDTH = 208
LANES = 256
VMEM = pl.BlockSpec(memory_space=pltpu.VMEM)
SMEM = pl.BlockSpec(memory_space=pltpu.SMEM)
HBM = pl.BlockSpec(memory_space=pltpu.HBM)
SMALL = pltpu.CompilerParams(vmem_limit_bytes=8 << 20)


def window_of(sizes_ref, irrep_ref, width):
    g = irrep_ref[0]
    first = jnp.int32(0)
    size = jnp.int32(0)
    for k in range(sizes_ref.shape[0]):
        first = first + jnp.where(k < g, sizes_ref[k], 0)
        size = size + jnp.where(k == g, sizes_ref[k], 0)
    start = jnp.minimum((first // 8) * 8, width - WIDTH)
    return first, first + size, start


def compact_kernel(irrep_ref, sizes_hbm, amps_hbm, compact_ref, sizes_ref, amps_ref, wide, sems):
    width = amps_hbm.shape[1]
    sizes_copy = pltpu.make_async_copy(sizes_hbm, sizes_ref, sems.at[0])
    amps_copy = pltpu.make_async_copy(amps_hbm, amps_ref, sems.at[1])
    sizes_copy.start()
    amps_copy.start()
    sizes_copy.wait()
    first, last, start = window_of(sizes_ref, irrep_ref, width)
    amps_copy.wait()
    wide[:, :width] = amps_ref[...].astype(jnp.float32)
    total = wide.shape[1]
    moved = pltpu.roll(wide[...], total - start, axis=1)[:, :LANES]
    d = lax.broadcasted_iota(jnp.int32, moved.shape, 1) + start
    moved = jnp.where((d >= first) & (d < last), moved, 0.0).astype(jnp.bfloat16)
    for j in range(compact_ref.shape[0]):
        compact_ref[j] = moved


def window_kernel(irrep_ref, sizes_hbm, ints_hbm, window_ref, sizes_ref, sems):
    sizes_copy = pltpu.make_async_copy(sizes_hbm, sizes_ref, sems.at[0])
    sizes_copy.start()
    sizes_copy.wait()
    _, _, start = window_of(sizes_ref, irrep_ref, ints_hbm.shape[0])
    window_copy = pltpu.make_async_copy(
        ints_hbm.at[pl.ds(pl.multiple_of(start, 8), WIDTH), :], window_ref, sems.at[1]
    )
    window_copy.start()
    window_copy.wait()


def spread_kernel(column_ref, halves_hbm, sems):
    copies = []
    for j in range(8):
        x_hi = ((j ^ X_FIRST) >> 1) & 1
        copies.append(pltpu.make_async_copy(column_ref.at[pl.ds(8 * x_hi, 8)], halves_hbm.at[j], sems.at[j]))
        copies[-1].start()
    for copy in copies:
        copy.wait()


def encode(values):
    top = jnp.max(jnp.abs(values), axis=1, keepdims=True)
    eighths = jnp.ceil(jnp.log2(jnp.maximum(top, 1e-33)) * 8.0) + 1.0
    scaled = values * (32767.0 * jnp.exp2(eighths * -0.125))
    return jnp.round(scaled).astype(jnp.int32).astype(jnp.int16), eighths


def multiply_kernel(rows_ref, own_ref, other_ref, coded_ref):
    me = lax.axis_index("x_hi")
    total = None
    for side, ints in ((me, own_ref), (1 - me, other_ref)):
        pieces = [
            rows_ref[((x_lo * 4 + core) ^ X_FIRST) ^ (2 * side), (2 * q + low + 1) % 8]
            for x_lo in range(2)
            for q in range(4)
            for low in range(2)
            for core in range(2)
        ]
        rows = jnp.concatenate(pieces, axis=0)[:, :WIDTH]
        term = jnp.dot(rows, ints[...], preferred_element_type=jnp.float32)
        total = term if total is None else total + term
    codes, eighths = encode(total)
    share = total.shape[0] // 8
    tiles = total.shape[1] // 128
    for y in range(8):
        scales = jnp.zeros((8, 128), jnp.float32)
        lane = lax.broadcasted_iota(jnp.int32, (8, 128), 1) // 32
        for t in range(share // 8):
            at = y * share + t * 8
            for u in range(tiles):
                coded_ref[Y_ORDER.index(y), pl.ds((t * tiles + u) * 8, 8), :] = codes[at : at + 8, u * 128 : (u + 1) * 128]
            scales = jnp.where(lane == t, eighths[at : at + 8], scales)
        coded_ref[Y_ORDER.index(y), pl.ds(share * tiles, 8), :] = scales.astype(jnp.int32).astype(jnp.int16)


def add_kernel(coded_ref, out_hbm, out_ref, sems):
    share, columns = out_ref.shape
    tiles = columns // 128
    scales = []
    for s in range(coded_ref.shape[0]):
        marks = coded_ref[s, pl.ds(share * tiles, 8), :].astype(jnp.int32).astype(jnp.float32)
        scales.append(jnp.exp2(marks * 0.125) * (1.0 / 32767.0))
    copies = []
    for t in range(share // 8):
        totals = [None] * tiles
        for s, marks in enumerate(scales):
            scale = marks[:, t * 32 : t * 32 + 1]
            for u in range(tiles):
                part = coded_ref[s, pl.ds((t * tiles + u) * 8, 8), :]
                part = part.astype(jnp.int32).astype(jnp.float32) * scale
                totals[u] = part if totals[u] is None else totals[u] + part
        for u, value in enumerate(totals):
            out_ref[pl.ds(t * 8, 8), pl.ds(u * 128, 128)] = value
        rows = pl.ds(t * 8, 8)
        copies.append(pltpu.make_async_copy(out_ref.at[rows], out_hbm.at[rows], sems.at[t]))
        copies[-1].start()
    for copy in copies:
        copy.wait()


def exchange(x, axis, order):
    return lax.all_to_all(x, axis, 0, 0, axis_index_groups=[order], tiled=True)


def body(amps, integrals, irrep_sizes, c_irreps):
    n, _, width = amps.shape
    columns = integrals.shape[0]
    amps = amps.reshape(n, width)
    ints = jnp.transpose(integrals.reshape(columns, width))
    sizes, amps, ints = (pltpu.with_memory_space_constraint(a, pltpu.HBM) for a in (irrep_sizes, amps, ints))
    compact = pl.pallas_call(
        compact_kernel,
        out_shape=jax.ShapeDtypeStruct((16, n, LANES), jnp.bfloat16),
        in_specs=[SMEM, HBM, HBM],
        out_specs=VMEM,
        scratch_shapes=[
            pltpu.SMEM(irrep_sizes.shape, jnp.int32),
            pltpu.VMEM(amps.shape, amps.dtype),
            pltpu.VMEM((n, 1024), jnp.float32),
            pltpu.SemaphoreType.DMA((2,)),
        ],
        compiler_params=SMALL,
        name="compact",
    )(c_irreps, sizes, amps)
    window = pl.pallas_call(
        window_kernel,
        out_shape=jax.ShapeDtypeStruct((WIDTH, columns), jnp.bfloat16),
        in_specs=[SMEM, HBM, HBM],
        out_specs=VMEM,
        scratch_shapes=[pltpu.SMEM(irrep_sizes.shape, jnp.int32), pltpu.SemaphoreType.DMA((2,))],
        compiler_params=SMALL,
        name="window",
    )(c_irreps, sizes, ints)
    other = lax.ppermute(window, "x_hi", [(0, 1), (1, 0)])
    column = exchange(compact, "z", Z_ORDER)
    halves = pl.pallas_call(
        spread_kernel,
        out_shape=jax.ShapeDtypeStruct((8, 8, n, LANES), jnp.bfloat16),
        in_specs=[VMEM],
        out_specs=HBM,
        scratch_shapes=[pltpu.SemaphoreType.DMA((8,))],
        compiler_params=SMALL,
        name="spread",
    )(column)
    rows = exchange(halves, ("x_lo", "x_hi", "core"), [j ^ X_FIRST for j in range(8)])
    share = 32
    length = share * columns // 128 + 8
    coded = pl.pallas_call(
        multiply_kernel,
        out_shape=jax.ShapeDtypeStruct((8, length, 128), jnp.int16),
        in_specs=[VMEM, VMEM, VMEM],
        out_specs=VMEM,
        compiler_params=SMALL,
        name="multiply",
    )(rows, window, other)
    coded = exchange(coded, "y", Y_ORDER)
    return pl.pallas_call(
        add_kernel,
        out_shape=jax.ShapeDtypeStruct((share, columns), jnp.float32),
        in_specs=[VMEM],
        out_specs=HBM,
        scratch_shapes=[pltpu.VMEM((share, columns), jnp.float32), pltpu.SemaphoreType.DMA((share // 8,))],
        compiler_params=SMALL,
        name="add",
    )(coded)


def solution(mesh):
    fine = Mesh(mesh.devices.reshape(2, 16, 2, 8, 2), ("x_lo", "z", "core", "y", "x_hi"))
    amp, inter = ("x_lo", "z", "core"), ("y", "x_hi")
    placed = (P(amp, inter, None), P(amp, inter, None), P(), P(inter))
    return jax.shard_map(
        body, mesh=fine, in_specs=placed, out_specs=P(inter, amp), check_vma=False
    )
```
